32 devices in a mesh: dp: 2 (over core), tm: 4 (over y, x), space: 4 (over z).
Axes of the slice: x: 2, y: 2, z: 4, core: 2. Of those that a mesh axis runs over, the one named last changes fastest.
Arguments:
- features: bfloat16 [2, 8, 32, 64, 512], P('dp', 'tm', 'space'), may hold values from -60 to 60
- base_spatial: bfloat16 [4608, 512], P('dp'), may hold values from -0.09375 to 0.09375
- delta_spatial: bfloat16 [4608, 512], P('dp'), may hold values from -0.09375 to 0.09375
- keep_spatial: int32 [4608, 512], P('dp'), may hold values 0 or 1
- base_temporal: bfloat16 [1536, 512], P('dp'), may hold values from -0.15625 to 0.15625
- delta_temporal: bfloat16 [1536, 512], P('dp'), may hold values from -0.15625 to 0.15625
- keep_temporal: int32 [1536, 512], P('dp'), may hold values 0 or 1
- cotangent: bfloat16 [2, 8, 32, 64, 512], P('dp', 'tm', 'space'), may hold values from -60 to 60
Outputs:
- decoded: bfloat16 [2, 8, 32, 64, 512], P('dp', 'tm', 'space')
- grad_input: bfloat16 [2, 8, 32, 64, 512], P('dp', 'tm', 'space')
- grad_spatial: float32 [4608, 512], P(('dp', 'tm', 'space'))
- grad_temporal: float32 [1536, 512], P(('dp', 'tm', 'space'))
The draws below stay inside these ranges and needn't reach their ends.
All inputs are finite; a program needn't handle non-finite values. No bound on the sum of `keep_spatial` or of `keep_temporal` on one device may be relied on, other than what follows from the above.
Results may differ from the reference program's by a relative error of at most 0.008.
Values may be sent and summed in bfloat16 or wider, within the bound.
A program may use at most 128 MiB of HBM per device.

```python
import math
import jax
import jax.numpy as jnp
from jax import lax

C = 512
GROUPS = 32
WIDTH = 64
CLIPS = 2
NF = 8
NH = 32


def rising_profile(frame_total, row_total):
    frame_pos = jnp.arange(frame_total, dtype=jnp.float32) / max(frame_total - 1, 1)
    row_pos = jnp.arange(row_total, dtype=jnp.float32) / max(row_total - 1, 1)
    return jnp.exp(0.5 * jnp.log(3.0) * (frame_pos[:, None] + row_pos[None, :]))


def field_draw(key, salt_value):
    keys_all = jax.random.split(jax.random.fold_in(key, salt_value), 3)
    shape_all = (CLIPS, NF, NH, WIDTH, C)
    chan_scale = jnp.exp(jax.random.uniform(keys_all[1], (CLIPS, 1, 1, 1, C), minval=jnp.log(0.3), maxval=jnp.log(3.0)))
    chan_shift = jax.random.uniform(keys_all[2], (CLIPS, 1, 1, 1, C), minval=-1.0, maxval=1.0)
    rising = rising_profile(NF, NH)[None, :, :, None, None]
    core_part = jax.random.truncated_normal(keys_all[0], -4.0, 4.0, shape_all)
    return ((core_part + chan_shift) * chan_scale * rising).astype(jnp.bfloat16)


def draw_features(key, part):
    return field_draw(key, 11)


def draw_cotangent(key, part):
    return field_draw(key, 23)


def plant(result, rng, low, high):
    place = [jax.random.randint(jax.random.fold_in(rng, axis), (), 0, length) for axis, length in enumerate(result.shape)]
    widest = result.shape.index(max(result.shape))
    beside = place[:widest] + [(place[widest] + 1) % result.shape[widest]] + place[widest + 1:]
    return result.at[tuple(place)].set(low).at[tuple(beside)].set(high)


def levels(key, extent, shards, least, largest):
    def one(dim, shards_of):
        draws = jax.random.uniform(jax.random.fold_in(jax.random.fold_in(key, 6), dim), (shards_of,), jnp.float32, least / len(shards), largest / len(shards))
        return jnp.repeat(jnp.exp(draws), extent[dim] // shards_of).reshape((-1,) + (1,) * (len(extent) - dim - 1))

    factor_of = one(*shards[0])
    for cut in shards[1:]:
        factor_of = factor_of * one(*cut)
    return factor_of


def noise(rng, dims, scale, most, cuts=(), held_as=jnp.bfloat16):
    gain = levels(rng, dims, cuts, -0.22, 0.18) if cuts else 1.0
    drawn = jax.random.normal(rng, dims, jnp.float32) * scale * gain
    return jnp.minimum(jnp.maximum(drawn, -most), most).astype(held_as)


def setup_inputs(seed: int = 0) -> dict:
    streams_of = jax.random.split(jax.random.key(seed), 9)
    return {
        "features": draw_features(jax.random.fold_in(streams_of[8], 71), 0),
        "base_spatial": noise(streams_of[1], (9 * C, C), (9 * C) ** -0.5, 0.09375, ((0, 2),)),
        "delta_spatial": noise(streams_of[2], (9 * C, C), (9 * C) ** -0.5, 0.09375, ((0, 2),)),
        "keep_spatial": plant((jax.random.randint(streams_of[3], (9 * C, C), 0, 5) < 4).astype(jnp.int32), jax.random.fold_in(streams_of[3], 1), 0, 1),
        "base_temporal": noise(streams_of[4], (3 * C, C), (3 * C) ** -0.5, 0.15625, ((0, 2),)),
        "delta_temporal": noise(streams_of[5], (3 * C, C), (3 * C) ** -0.5, 0.15625, ((0, 2),)),
        "keep_temporal": plant((jax.random.randint(streams_of[6], (3 * C, C), 0, 5) < 4).astype(jnp.int32), jax.random.fold_in(streams_of[6], 1), 0, 1),
        "cotangent": draw_cotangent(jax.random.fold_in(streams_of[8], 71), 0),
    }


EPS = 1e-06

def conv_frames(padded, kernel, layout):
    return lax.conv_general_dilated(padded, kernel, (1, 1), 'VALID', dimension_numbers=('NHWC', layout, 'NHWC'), precision=lax.Precision.HIGHEST)

def norm_forward(field, group_size):
    values = field.astype(jnp.float32)
    channels = values.shape[-1]
    grouped = values.reshape(values.shape[:-1] + (GROUPS, channels // GROUPS))
    average = lax.optimization_barrier(jnp.sum(grouped, axis=(0, 1, 2, 4))) / group_size
    centered = grouped - average[:, None]
    variance = lax.optimization_barrier(jnp.sum(centered * centered, axis=(0, 1, 2, 4))) / group_size
    inverse_dev = lax.rsqrt(variance + EPS)
    return ((centered * inverse_dev[:, None]).reshape(values.shape), inverse_dev)

def norm_backward(upstream, normed, inverse_dev, group_size):
    channels = normed.shape[-1]
    sigmoid_val = jax.nn.sigmoid(normed)
    slope_grad = upstream * sigmoid_val * (1.0 + normed * (1.0 - sigmoid_val))
    new_shape = slope_grad.shape[:-1] + (GROUPS, channels // GROUPS)
    grouped_grad = slope_grad.reshape(new_shape)
    grouped_norm = normed.reshape(new_shape)
    sum_grad = lax.optimization_barrier(jnp.sum(grouped_grad, axis=(0, 1, 2, 4))) / group_size
    sum_cross = lax.optimization_barrier(jnp.sum(grouped_grad * grouped_norm, axis=(0, 1, 2, 4))) / group_size
    result_grad = (grouped_grad - sum_grad[:, None] - grouped_norm * sum_cross[:, None]) * inverse_dev[:, None]
    return result_grad.reshape(slope_grad.shape)

def one_clip(features, cotangent, kernel_space, kernel_time, group_size):
    frames = features.shape[0]
    row_count = features.shape[1]
    col_count = features.shape[2]
    normed_in, inverse_in = norm_forward(features, group_size)
    activated = jax.nn.silu(normed_in).astype(jnp.bfloat16)
    padded_act = jnp.pad(activated.astype(jnp.float32), ((0, 0), (1, 1), (1, 1), (0, 0)))
    space_wide = kernel_space.astype(jnp.float32)
    hidden = conv_frames(padded_act, space_wide, 'HWIO').astype(jnp.bfloat16)
    normed_mid, inverse_mid = norm_forward(hidden, group_size)
    gated_act = jax.nn.silu(normed_mid).astype(jnp.bfloat16)
    gated_wide = gated_act.astype(jnp.float32)
    extended = jnp.concatenate([gated_wide[0:1], gated_wide[0:1], gated_wide], axis=0)
    time_wide = kernel_time.astype(jnp.float32)
    output = jnp.zeros(gated_wide.shape, jnp.float32)
    for tap_index in range(3):
        output = output + jnp.einsum('fhwc,cd->fhwd', extended[tap_index:tap_index + frames], time_wide[tap_index], precision=lax.Precision.HIGHEST)
    decoded = output.astype(jnp.bfloat16)
    upstream = cotangent.astype(jnp.float32)
    pad_grad = jnp.zeros((frames + 2,) + upstream.shape[1:], jnp.float32)
    time_grads = []
    for tap_index in range(3):
        pad_grad = pad_grad.at[tap_index:tap_index + frames].add(jnp.einsum('fhwd,cd->fhwc', upstream, time_wide[tap_index], precision=lax.Precision.HIGHEST))
        time_grads.append(jnp.einsum('fhwc,fhwd->cd', extended[tap_index:tap_index + frames], upstream, precision=lax.Precision.HIGHEST))
    grad_gated = pad_grad[2:].at[0].add(pad_grad[0] + pad_grad[1])
    grad_hidden = norm_backward(grad_gated, normed_mid, inverse_mid, group_size).astype(jnp.bfloat16)
    hidden_wide = grad_hidden.astype(jnp.float32)
    space_grads = []
    for row_shift in range(3):
        for col_shift in range(3):
            window = padded_act[:, row_shift:row_shift + row_count, col_shift:col_shift + col_count, :]
            space_grads.append(jnp.einsum('fhwc,fhwd->cd', window, hidden_wide, precision=lax.Precision.HIGHEST))
    padded_grad = jnp.pad(hidden_wide, ((0, 0), (1, 1), (1, 1), (0, 0)))
    grad_act = conv_frames(padded_grad, jnp.flip(space_wide, axis=(0, 1)), 'HWOI')
    grad_input = norm_backward(grad_act, normed_in, inverse_in, group_size).astype(jnp.bfloat16)
    return (decoded, grad_input, jnp.concatenate(space_grads, axis=0), jnp.concatenate(time_grads, axis=0))

def reference(features, base_spatial, delta_spatial, keep_spatial, base_temporal, delta_temporal, keep_temporal, cotangent):
    merged_spatial = (base_spatial.astype(jnp.float32) + keep_spatial.astype(jnp.float32) * delta_spatial.astype(jnp.float32)).astype(jnp.bfloat16)
    merged_temporal = (base_temporal.astype(jnp.float32) + keep_temporal.astype(jnp.float32) * delta_temporal.astype(jnp.float32)).astype(jnp.bfloat16)
    kernel_space = merged_spatial.reshape(3, 3, C, C)
    kernel_time = merged_temporal.reshape(3, C, C)
    group_size = float(NF * NH * WIDTH * (C // GROUPS))
    grad_factor = 1.0 / math.sqrt(CLIPS * NF * NH * WIDTH)
    decoded_list = []
    input_list = []
    grad_spatial = jnp.zeros((9 * C, C), jnp.float32)
    grad_temporal = jnp.zeros((3 * C, C), jnp.float32)
    for clip_index in range(CLIPS):
        clip_result = one_clip(features[clip_index], cotangent[clip_index], kernel_space, kernel_time, group_size)
        decoded_list.append(clip_result[0])
        input_list.append(clip_result[1])
        grad_spatial = grad_spatial + clip_result[2]
        grad_temporal = grad_temporal + clip_result[3]
    return (jnp.stack(decoded_list), jnp.stack(input_list), grad_spatial * grad_factor, grad_temporal * grad_factor)
```

```python
import functools
import math

import jax
import jax.numpy as jnp
from jax import lax
from jax.experimental import pallas as pl
from jax.experimental.pallas import tpu as pltpu
from jax.sharding import PartitionSpec as P

LANES = 128
MESH = pl.DeviceIdType.MESH

GROUPS = 32


EPS = 1e-06


def passed_along(x, axis, by):
    peers = lax.axis_size(axis)
    pairs = [(i, i + by) for i in range(peers) if 0 <= i + by < peers]
    return lax.ppermute(x, axis, pairs)


def padded_2(x, sides, width):
    for axis, dim in sides:
        peers, length = (lax.axis_size(axis), x.shape[dim])
        up = [(i, (i + 1) % peers) for i in range(peers - 1)]
        down = [(j, i) for i, j in up]
        last = lax.slice_in_dim(x, length - width, length, axis=dim)
        initial = lax.slice_in_dim(x, 0, width, axis=dim)
        before = lax.ppermute(last, axis, up)
        after = lax.ppermute(initial, axis, down)
        x = jnp.concatenate([before, x, after], axis=dim)
    return x


def sum_kernel(tm_size, space_size, width, x_ref, o_ref, slots, send_sems, recv_sems):
    peers = tm_size * space_size
    me = lax.axis_index("tm") * space_size + lax.axis_index("space")

    def place(step):
        peer = lax.rem(me + step, peers)
        return {"tm": peer // space_size, "space": lax.rem(peer, space_size)}

    barrier = pltpu.get_barrier_semaphore()
    for step in range(1, peers):
        pl.semaphore_signal(barrier, inc=1, device_id=place(step), device_id_type=MESH)
    pl.semaphore_wait(barrier, peers - 1)
    copies = []
    for step in range(1, peers):
        copy = pltpu.make_async_remote_copy(
            src_ref=x_ref,
            dst_ref=slots.at[step],
            send_sem=send_sems.at[step],
            recv_sem=recv_sems.at[step],
            device_id=place(step),
            device_id_type=MESH,
        )
        copy.start()
        copies.append(copy)
    total = x_ref[...]
    for step, copy in enumerate(copies, 1):
        copy.wait_recv()
        total = total + slots[step]
    rows = lax.broadcasted_iota(jnp.int32, (LANES, LANES), 0)
    cols = lax.broadcasted_iota(jnp.int32, (LANES, LANES), 1)
    same = (rows // width == cols // width).astype(jnp.float32)
    o_ref[...] = jnp.dot(
        total, same, precision=lax.Precision.HIGHEST, preferred_element_type=jnp.float32
    )
    for copy in copies:
        copy.wait_send()


def group_sums(first, second):
    channels = first.shape[0]
    packed = jnp.concatenate([first.reshape(-1, LANES), second.reshape(-1, LANES)], axis=0)
    tm_size, space_size = lax.axis_size("tm"), lax.axis_size("space")
    peers = tm_size * space_size
    sums = pl.pallas_call(
        functools.partial(sum_kernel, tm_size, space_size, channels // GROUPS),
        out_shape=jax.ShapeDtypeStruct(packed.shape, jnp.float32),
        in_specs=[pl.BlockSpec(memory_space=pltpu.VMEM)],
        out_specs=pl.BlockSpec(memory_space=pltpu.VMEM),
        scratch_shapes=[
            pltpu.VMEM((peers,) + packed.shape, jnp.float32),
            pltpu.SemaphoreType.DMA((peers,)),
            pltpu.SemaphoreType.DMA((peers,)),
        ],
        compiler_params=pltpu.CompilerParams(collective_id=0, has_side_effects=True),
    )(packed)
    half = packed.shape[0] // 2
    return sums[:half].reshape(channels), sums[half:].reshape(channels)


def both_halves(mine):
    if lax.axis_size("dp") != 2:
        return lax.all_gather(mine, "dp", axis=0, tiled=True)
    other = lax.ppermute(mine, "dp", [(0, 1), (1, 0)])
    initial = lax.axis_index("dp") == 0
    return jnp.concatenate(
        [jnp.where(initial, mine, other), jnp.where(initial, other, mine)], axis=0
    )


def axis_bits(axis):
    size = lax.axis_size(axis)
    return [(axis, bit) for bit in reversed(range(size.bit_length() - 1))]


def scattered(terms, order):
    bits = axis_bits("dp") + axis_bits("tm") + axis_bits("space")
    rows, cols = terms.shape
    total = terms.reshape((2,) * len(bits) + (rows >> len(bits), cols))
    left = list(bits)
    for axis, bit in order:
        dim = left.index((axis, bit))
        left.pop(dim)
        mine = (lax.axis_index(axis) >> bit) & 1
        kept = lax.dynamic_index_in_dim(total, mine, dim, keepdims=False)
        sent = lax.dynamic_index_in_dim(total, 1 - mine, dim, keepdims=False)
        pairs = [(i, i ^ (1 << bit)) for i in range(lax.axis_size(axis))]
        got = lax.ppermute(sent.astype(jnp.bfloat16), axis, pairs)
        total = kept + got.astype(jnp.float32)
    return total


def reduce_rows(terms):
    near = list(reversed(axis_bits("space")))
    tm_bits = axis_bits("tm")
    first = axis_bits("dp") + tm_bits + near
    second = axis_bits("dp") + tm_bits[::-1] + near
    return jnp.concatenate(
        [scattered(terms[0], first), scattered(terms[1], second)], axis=1
    )


def along_time(edge_frames, offset):
    return passed_along(edge_frames, "tm", offset)


def rows_around(field):
    padded = padded_2(field, (("space", 1),), 1)
    return jnp.pad(padded, ((0, 0), (0, 0), (1, 1), (0, 0)))


def conv_frames(padded, kernel, layout):
    return lax.conv_general_dilated(
        padded,
        kernel,
        (1, 1),
        "VALID",
        dimension_numbers=("NHWC", layout, "NHWC"),
        preferred_element_type=jnp.float32,
    )


def against_rows(left_rows, kernel):
    return lax.dot_general(
        left_rows, kernel, (((1,), (1,)), ((), ())), preferred_element_type=jnp.float32
    )


def over_pixels(left_rows, right_rows):
    return lax.dot_general(
        left_rows, right_rows, (((0,), (0,)), ((), ())), preferred_element_type=jnp.float32
    )


def norm_stats(field, group_size):
    values = field.astype(jnp.float32)
    total, square_sum = group_sums(
        jnp.sum(values, axis=(0, 1, 2)), jnp.sum(values * values, axis=(0, 1, 2))
    )
    average = total / group_size
    variance = square_sum / group_size - average * average
    inverse_dev = lax.rsqrt(variance + EPS)
    normed = (values - average) * inverse_dev
    return (normed, inverse_dev)


def norm_backward(upstream, normed, inverse_dev, group_size):
    sigmoid_val = jax.nn.sigmoid(normed)
    slope_grad = upstream * sigmoid_val * (1.0 + normed * (1.0 - sigmoid_val))
    sum_grad, sum_cross = group_sums(
        jnp.sum(slope_grad, axis=(0, 1, 2)), jnp.sum(slope_grad * normed, axis=(0, 1, 2))
    )
    centered = slope_grad - sum_grad / group_size - normed * (sum_cross / group_size)
    return centered * inverse_dev


def kernel_grads(windows, flat):
    half = flat.shape[1] // 2
    parts = [
        jnp.concatenate([over_pixels(window, side) for window in windows], axis=0)
        for side in (flat[:, :half], flat[:, half:])
    ]
    return reduce_rows(parts)


def local(
    features,
    base_spatial,
    delta_spatial,
    keep_spatial,
    base_temporal,
    delta_temporal,
    keep_temporal,
    cotangent,
):
    frames, row_count, col_count, channels = (
        features.shape[1],
        features.shape[2],
        features.shape[3],
        features.shape[4],
    )
    spread_over = lax.axis_size("tm") * lax.axis_size("space")
    group_size = float(frames * row_count * col_count * spread_over * (channels // GROUPS))
    pixels = frames * row_count * col_count
    grad_factor = 1.0 / math.sqrt(pixels * spread_over * lax.axis_size("dp"))
    merged_spatial = (
        base_spatial.astype(jnp.float32)
        + keep_spatial.astype(jnp.float32) * delta_spatial.astype(jnp.float32)
    ).astype(jnp.bfloat16)
    merged_temporal = (
        base_temporal.astype(jnp.float32)
        + keep_temporal.astype(jnp.float32) * delta_temporal.astype(jnp.float32)
    ).astype(jnp.bfloat16)
    full_spatial, full_temporal = both_halves(merged_spatial), both_halves(merged_temporal)
    kernel_space = full_spatial.reshape(3, 3, channels, channels)
    kernel_time = full_temporal.reshape(3, channels, channels)
    inputs = features[0]
    normed_in, inverse_in = norm_stats(inputs, group_size)
    activated = jax.nn.silu(normed_in).astype(jnp.bfloat16)
    padded_act = rows_around(activated)
    hidden = conv_frames(padded_act, kernel_space, "HWIO").astype(jnp.bfloat16)
    normed_mid, inverse_mid = norm_stats(hidden, group_size)
    gated_act = jax.nn.silu(normed_mid).astype(jnp.bfloat16)
    leading = lax.axis_index("tm") == 0
    earlier = along_time(gated_act[frames - 2 :], 1)
    earlier = jnp.where(leading, jnp.broadcast_to(gated_act[0:1], earlier.shape), earlier)
    extended = jnp.concatenate([earlier, gated_act], axis=0).reshape(
        frames + 2, row_count * col_count, channels
    )
    output = jnp.zeros((pixels, channels), jnp.float32)
    for tap_index in range(3):
        output = output + jnp.dot(
            extended[tap_index : tap_index + frames].reshape(pixels, channels),
            kernel_time[tap_index],
            preferred_element_type=jnp.float32,
        )
    decoded = output.reshape(frames, row_count, col_count, channels).astype(jnp.bfloat16)[None]
    upstream = cotangent[0]
    later = along_time(upstream, -1)
    ahead = jnp.concatenate([upstream, later], axis=0).reshape(
        frames + 2, row_count * col_count, channels
    )
    flat_up = upstream.reshape(pixels, channels)
    grad_gated = jnp.zeros((pixels, channels), jnp.float32)
    time_grads = []
    for tap_index in range(3):
        grad_gated = grad_gated + against_rows(
            ahead[2 - tap_index : 2 - tap_index + frames].reshape(pixels, channels),
            kernel_time[tap_index],
        )
        time_grads.append(extended[tap_index : tap_index + frames].reshape(pixels, channels))
    edge_rows = row_count * col_count
    first_up = flat_up[:edge_rows]
    second_up = flat_up[edge_rows : 2 * edge_rows]
    edge_term = (
        against_rows(first_up, kernel_time[0])
        + against_rows(second_up, kernel_time[0])
        + against_rows(first_up, kernel_time[1])
    )
    edge_term = jnp.where(leading, edge_term, 0.0)
    grad_gated = jnp.concatenate(
        [grad_gated[:edge_rows] + edge_term, grad_gated[edge_rows:]], axis=0
    )
    grad_hidden = norm_backward(
        grad_gated.reshape(frames, row_count, col_count, channels),
        normed_mid,
        inverse_mid,
        group_size,
    ).astype(jnp.bfloat16)
    flat_hidden = grad_hidden.reshape(pixels, channels)
    space_grads = []
    for row_shift in range(3):
        for col_shift in range(3):
            window = padded_act[
                :, row_shift : row_shift + row_count, col_shift : col_shift + col_count, :
            ].reshape(pixels, channels)
            space_grads.append(window)
    grad_act = conv_frames(rows_around(grad_hidden), jnp.flip(kernel_space, axis=(0, 1)), "HWOI")
    grad_input = norm_backward(grad_act, normed_in, inverse_in, group_size).astype(jnp.bfloat16)[
        None
    ]
    grad_spatial = kernel_grads(space_grads, flat_hidden) * grad_factor
    grad_temporal = kernel_grads(time_grads, flat_up) * grad_factor
    return (decoded, grad_input, grad_spatial, grad_temporal)


def solution(mesh):
    placed = (
        P("dp", "tm", "space", None, None),
        P("dp", None),
        P("dp", None),
        P("dp", None),
        P("dp", None),
        P("dp", None),
        P("dp", None),
        P("dp", "tm", "space", None, None),
    )
    return jax.shard_map(
        local,
        mesh=mesh,
        in_specs=placed,
        out_specs=(
            P("dp", "tm", "space", None, None),
            P("dp", "tm", "space", None, None),
            P(("dp", "tm", "space"), None),
            P(("dp", "tm", "space"), None),
        ),
        check_vma=False,
    )
```

```python
import functools
import math

import jax
import jax.numpy as jnp
from jax import lax
from jax.experimental import pallas as pl
from jax.experimental.pallas import tpu as pltpu
from jax.sharding import PartitionSpec as P


LANES = 128
CHUNK = 32
MESH = pl.DeviceIdType.MESH

GROUPS = 32


EPS = 1e-06


def passed_along(x, axis, by):
    peers = lax.axis_size(axis)
    pairs = [(i, i + by) for i in range(peers) if 0 <= i + by < peers]
    return lax.ppermute(x, axis, pairs)


def padded_2(x, sides, width):
    for axis, dim in sides:
        peers, length = (lax.axis_size(axis), x.shape[dim])
        up = [(i, (i + 1) % peers) for i in range(peers - 1)]
        down = [(j, i) for i, j in up]
        last = lax.slice_in_dim(x, length - width, length, axis=dim)
        initial = lax.slice_in_dim(x, 0, width, axis=dim)
        before = lax.ppermute(last, axis, up)
        after = lax.ppermute(initial, axis, down)
        x = jnp.concatenate([before, x, after], axis=dim)
    return x


def greet(tm_size, space_size):
    peers = tm_size * space_size
    me = lax.axis_index("tm") * space_size + lax.axis_index("space")
    places = {}
    for step in range(1, peers):
        peer = lax.rem(me + step, peers)
        places[step] = {"tm": peer // space_size, "space": lax.rem(peer, space_size)}
    barrier = pltpu.get_barrier_semaphore()
    for place in places.values():
        pl.semaphore_signal(barrier, inc=1, device_id=place, device_id_type=MESH)
    return barrier, places


def clip_sums(barrier, places, width, packed, slots, send_sems, recv_sems):
    pl.semaphore_wait(barrier, len(places))
    copies = []
    for step, place in places.items():
        copy = pltpu.make_async_remote_copy(
            src_ref=packed,
            dst_ref=slots.at[step],
            send_sem=send_sems.at[step],
            recv_sem=recv_sems.at[step],
            device_id=place,
            device_id_type=MESH,
        )
        copy.start()
        copies.append((step, copy))
    rows = lax.broadcasted_iota(jnp.int32, (LANES, LANES), 0)
    cols = lax.broadcasted_iota(jnp.int32, (LANES, LANES), 1)
    same = (rows // width == cols // width).astype(jnp.float32)
    total = packed[...]
    for step, copy in copies:
        copy.wait_recv()
        total = total + slots[step]
    sums = jnp.concatenate(
        [
            jnp.dot(
                total[:, start : start + LANES],
                same,
                precision=lax.Precision.HIGHEST,
                preferred_element_type=jnp.float32,
            )
            for start in range(0, total.shape[1], LANES)
        ],
        axis=1,
    )
    for step, copy in copies:
        copy.wait_send()
    return sums[0:1], sums[1:2]


def folded(values):
    return jnp.sum(values.reshape(-1, 8, values.shape[-1]), axis=0)


def packed_sums(packed, first, second):
    packed[0:1] = jnp.sum(first, axis=0, keepdims=True)
    packed[1:2] = jnp.sum(second, axis=0, keepdims=True)


def norm_kernel(sizes, width, group_size, x_ref, act_ref, stat_ref, packed, slots, sends, recvs):
    barrier, places = greet(*sizes)
    pixels, channels = x_ref.shape
    steps = pixels // CHUNK
    zeros = jnp.zeros((8, channels), jnp.float32)

    def gather(step, carry):
        values = x_ref[pl.ds(step * CHUNK, CHUNK)].astype(jnp.float32)
        return carry[0] + folded(values), carry[1] + folded(values * values)

    packed_sums(packed, *lax.fori_loop(0, steps, gather, (zeros, zeros)))
    total, square_sum = clip_sums(barrier, places, width, packed, slots, sends, recvs)
    average = total / group_size
    inverse_dev = lax.rsqrt(square_sum / group_size - average * average + EPS)
    stat_ref[0:1] = average
    stat_ref[1:2] = inverse_dev

    def apply(step, carry):
        rows = pl.ds(step * CHUNK, CHUNK)
        normed = (x_ref[rows].astype(jnp.float32) - average) * inverse_dev
        act_ref[rows] = (normed * jax.nn.sigmoid(normed)).astype(jnp.bfloat16)
        return carry

    lax.fori_loop(0, steps, apply, 0)


def back_kernel(
    sizes, width, group_size, up_ref, x_ref, stat_ref, out_ref, slope, packed, slots, sends, recvs
):
    barrier, places = greet(*sizes)
    pixels, channels = x_ref.shape
    steps = pixels // CHUNK
    zeros = jnp.zeros((8, channels), jnp.float32)
    average = stat_ref[0:1]
    inverse_dev = stat_ref[1:2]

    def normed_rows(rows):
        return (x_ref[rows].astype(jnp.float32) - average) * inverse_dev

    def gather(step, carry):
        rows = pl.ds(step * CHUNK, CHUNK)
        normed = normed_rows(rows)
        sigmoid_val = jax.nn.sigmoid(normed)
        values = up_ref[rows] * sigmoid_val * (1.0 + normed * (1.0 - sigmoid_val))
        slope[rows] = values
        return carry[0] + folded(values), carry[1] + folded(values * normed)

    packed_sums(packed, *lax.fori_loop(0, steps, gather, (zeros, zeros)))
    sum_grad, sum_cross = clip_sums(barrier, places, width, packed, slots, sends, recvs)
    mean_grad = sum_grad / group_size
    mean_cross = sum_cross / group_size

    def apply(step, carry):
        rows = pl.ds(step * CHUNK, CHUNK)
        centered = slope[rows] - mean_grad - normed_rows(rows) * mean_cross
        out_ref[rows] = (centered * inverse_dev).astype(jnp.bfloat16)
        return carry

    lax.fori_loop(0, steps, apply, 0)


def norm_call(kernel, ident, group_size, operands, out_shape, scratch):
    channels = operands[0].shape[-1]
    sizes = (lax.axis_size("tm"), lax.axis_size("space"))
    peers = sizes[0] * sizes[1]
    return pl.pallas_call(
        functools.partial(kernel, sizes, channels // GROUPS, group_size),
        out_shape=out_shape,
        in_specs=[pl.BlockSpec(memory_space=pltpu.VMEM)] * len(operands),
        out_specs=jax.tree.map(lambda _: pl.BlockSpec(memory_space=pltpu.VMEM), out_shape),
        scratch_shapes=scratch
        + [
            pltpu.VMEM((2, channels), jnp.float32),
            pltpu.VMEM((peers, 2, channels), jnp.float32),
            pltpu.SemaphoreType.DMA((peers,)),
            pltpu.SemaphoreType.DMA((peers,)),
        ],
        compiler_params=pltpu.CompilerParams(collective_id=ident, has_side_effects=True),
    )(*operands)


def norm_forward(field, group_size):
    flat = field.reshape(-1, field.shape[-1])
    out = (
        jax.ShapeDtypeStruct(flat.shape, jnp.bfloat16),
        jax.ShapeDtypeStruct((2, flat.shape[1]), jnp.float32),
    )
    act, stats = norm_call(norm_kernel, 0, group_size, [flat], out, [])
    return act.reshape(field.shape), stats


def norm_backward(upstream, field, stats, group_size):
    flat = field.reshape(-1, field.shape[-1])
    out = jax.ShapeDtypeStruct(flat.shape, jnp.bfloat16)
    scratch = [pltpu.VMEM(flat.shape, jnp.float32)]
    operands = [upstream.reshape(flat.shape), flat, stats]
    grad = norm_call(back_kernel, 1, group_size, operands, out, scratch)
    return grad.reshape(field.shape)


def both_halves(mine):
    if lax.axis_size("dp") != 2:
        return lax.all_gather(mine, "dp", axis=0, tiled=True)
    other = lax.ppermute(mine, "dp", [(0, 1), (1, 0)])
    initial = lax.axis_index("dp") == 0
    return jnp.concatenate(
        [jnp.where(initial, mine, other), jnp.where(initial, other, mine)], axis=0
    )


def axis_bits(axis):
    size = lax.axis_size(axis)
    return [(axis, bit) for bit in reversed(range(size.bit_length() - 1))]


def scattered(terms, order):
    bits = axis_bits("dp") + axis_bits("tm") + axis_bits("space")
    rows, cols = terms.shape
    total = terms.reshape((2,) * len(bits) + (rows >> len(bits), cols))
    left = list(bits)
    for axis, bit in order:
        dim = left.index((axis, bit))
        left.pop(dim)
        mine = (lax.axis_index(axis) >> bit) & 1
        kept = lax.dynamic_index_in_dim(total, mine, dim, keepdims=False)
        sent = lax.dynamic_index_in_dim(total, 1 - mine, dim, keepdims=False)
        pairs = [(i, i ^ (1 << bit)) for i in range(lax.axis_size(axis))]
        got = lax.ppermute(sent.astype(jnp.bfloat16), axis, pairs)
        total = kept + got.astype(jnp.float32)
    return total


def reduce_rows(terms):
    near = list(reversed(axis_bits("space")))
    tm_bits = axis_bits("tm")
    first = axis_bits("dp") + tm_bits + near
    second = axis_bits("dp") + tm_bits[::-1] + near
    return jnp.concatenate([scattered(terms[0], first), scattered(terms[1], second)], axis=1)


def along_time(edge_frames, offset):
    return passed_along(edge_frames, "tm", offset)


def rows_around(field):
    padded = padded_2(field, (("space", 1),), 1)
    return jnp.pad(padded, ((0, 0), (0, 0), (1, 1), (0, 0)))


def conv_frames(padded, kernel, layout):
    return lax.conv_general_dilated(
        padded,
        kernel,
        (1, 1),
        "VALID",
        dimension_numbers=("NHWC", layout, "NHWC"),
        preferred_element_type=jnp.float32,
    )


def against_rows(left_rows, kernel):
    return lax.dot_general(
        left_rows, kernel, (((1,), (1,)), ((), ())), preferred_element_type=jnp.float32
    )


def over_pixels(left_rows, right_rows):
    return lax.dot_general(
        left_rows, right_rows, (((0,), (0,)), ((), ())), preferred_element_type=jnp.float32
    )


def kernel_grads(windows, flat):
    half = flat.shape[1] // 2
    terms = jnp.concatenate([over_pixels(window, flat) for window in windows], axis=0)
    return reduce_rows((terms[:, :half], terms[:, half:]))


def local(
    features,
    base_spatial,
    delta_spatial,
    keep_spatial,
    base_temporal,
    delta_temporal,
    keep_temporal,
    cotangent,
):
    frames, row_count, col_count, channels = (
        features.shape[1],
        features.shape[2],
        features.shape[3],
        features.shape[4],
    )
    spread_over = lax.axis_size("tm") * lax.axis_size("space")
    group_size = float(frames * row_count * col_count * spread_over * (channels // GROUPS))
    pixels = frames * row_count * col_count
    grad_factor = 1.0 / math.sqrt(pixels * spread_over * lax.axis_size("dp"))
    merged_spatial = (
        base_spatial.astype(jnp.float32)
        + keep_spatial.astype(jnp.float32) * delta_spatial.astype(jnp.float32)
    ).astype(jnp.bfloat16)
    merged_temporal = (
        base_temporal.astype(jnp.float32)
        + keep_temporal.astype(jnp.float32) * delta_temporal.astype(jnp.float32)
    ).astype(jnp.bfloat16)
    full_spatial, full_temporal = both_halves(merged_spatial), both_halves(merged_temporal)
    kernel_space = full_spatial.reshape(3, 3, channels, channels)
    kernel_time = full_temporal.reshape(3, channels, channels)
    inputs = features[0]
    activated, stats_in = norm_forward(inputs, group_size)
    padded_act = rows_around(activated)
    shifted = [padded_act[:, :, shift : shift + col_count] for shift in range(3)]
    hidden = conv_frames(padded_act, kernel_space, "HWIO").astype(jnp.bfloat16)
    gated_act, stats_mid = norm_forward(hidden, group_size)
    leading = lax.axis_index("tm") == 0
    earlier = along_time(gated_act[frames - 2 :], 1)
    earlier = jnp.where(leading, jnp.broadcast_to(gated_act[0:1], earlier.shape), earlier)
    extended = jnp.concatenate([earlier, gated_act], axis=0).reshape(
        frames + 2, row_count * col_count, channels
    )
    output = jnp.zeros((pixels, channels), jnp.float32)
    for tap_index in range(3):
        output = output + jnp.dot(
            extended[tap_index : tap_index + frames].reshape(pixels, channels),
            kernel_time[tap_index],
            preferred_element_type=jnp.float32,
        )
    decoded = output.reshape(frames, row_count, col_count, channels).astype(jnp.bfloat16)[None]
    upstream = cotangent[0]
    later = along_time(upstream, -1)
    ahead = jnp.concatenate([upstream, later], axis=0).reshape(
        frames + 2, row_count * col_count, channels
    )
    flat_up = upstream.reshape(pixels, channels)
    grad_gated = jnp.zeros((pixels, channels), jnp.float32)
    time_grads = []
    for tap_index in range(3):
        grad_gated = grad_gated + against_rows(
            ahead[2 - tap_index : 2 - tap_index + frames].reshape(pixels, channels),
            kernel_time[tap_index],
        )
        time_grads.append(extended[tap_index : tap_index + frames].reshape(pixels, channels))
    edge_rows = row_count * col_count
    first_up = flat_up[:edge_rows]
    second_up = flat_up[edge_rows : 2 * edge_rows]
    edge_term = (
        against_rows(first_up, kernel_time[0])
        + against_rows(second_up, kernel_time[0])
        + against_rows(first_up, kernel_time[1])
    )
    edge_term = jnp.where(leading, edge_term, 0.0)
    grad_gated = jnp.concatenate(
        [grad_gated[:edge_rows] + edge_term, grad_gated[edge_rows:]], axis=0
    )
    grad_hidden = norm_backward(
        grad_gated.reshape(frames, row_count, col_count, channels), hidden, stats_mid, group_size
    )
    flat_hidden = grad_hidden.reshape(pixels, channels)
    space_grads = []
    for row_shift in range(3):
        for col_shift in range(3):
            window = shifted[col_shift][:, row_shift : row_shift + row_count]
            space_grads.append(window.reshape(pixels, channels))
    padded_grad = rows_around(grad_hidden)
    grad_act = conv_frames(padded_grad, jnp.flip(kernel_space, axis=(0, 1)), "HWOI")
    grad_input = norm_backward(grad_act, inputs, stats_in, group_size)[None]
    grad_spatial = kernel_grads(space_grads, flat_hidden) * grad_factor
    grad_temporal = kernel_grads(time_grads, flat_up) * grad_factor
    return (decoded, grad_input, grad_spatial, grad_temporal)


def solution(mesh):
    placed = (
        P("dp", "tm", "space", None, None),
        P("dp", None),
        P("dp", None),
        P("dp", None),
        P("dp", None),
        P("dp", None),
        P("dp", None),
        P("dp", "tm", "space", None, None),
    )
    return jax.shard_map(
        local,
        mesh=mesh,
        in_specs=placed,
        out_specs=(
            P("dp", "tm", "space", None, None),
            P("dp", "tm", "space", None, None),
            P(("dp", "tm", "space"), None),
            P(("dp", "tm", "space"), None),
        ),
        check_vma=False,
    )
```

```python
import functools
import math

import jax
import jax.numpy as jnp
from jax import lax
from jax.experimental import pallas as pl
from jax.experimental.pallas import tpu as pltpu
from jax.sharding import PartitionSpec as P


LANES = 128
CHUNK = 32
MESH = pl.DeviceIdType.MESH

GROUPS = 32


EPS = 1e-06


def passed_along(x, axis, by):
    peers = lax.axis_size(axis)
    pairs = [(i, i + by) for i in range(peers) if 0 <= i + by < peers]
    return lax.ppermute(x, axis, pairs)


def greet(tm_size, space_size):
    peers = tm_size * space_size
    me = lax.axis_index("tm") * space_size + lax.axis_index("space")
    places = {}
    for step in range(1, peers):
        peer = lax.rem(me + step, peers)
        places[step] = {"tm": peer // space_size, "space": lax.rem(peer, space_size)}
    barrier = pltpu.get_barrier_semaphore()
    for place in places.values():
        pl.semaphore_signal(barrier, inc=1, device_id=place, device_id_type=MESH)
    return barrier, places


def clip_sums(barrier, places, width, packed, slots, send_sems, recv_sems):
    pl.semaphore_wait(barrier, len(places))
    copies = []
    for step, place in places.items():
        copy = pltpu.make_async_remote_copy(
            src_ref=packed,
            dst_ref=slots.at[step],
            send_sem=send_sems.at[step],
            recv_sem=recv_sems.at[step],
            device_id=place,
            device_id_type=MESH,
        )
        copy.start()
        copies.append((step, copy))
    rows = lax.broadcasted_iota(jnp.int32, (LANES, LANES), 0)
    cols = lax.broadcasted_iota(jnp.int32, (LANES, LANES), 1)
    same = (rows // width == cols // width).astype(jnp.float32)
    total = packed[...]
    for step, copy in copies:
        copy.wait_recv()
        total = total + slots[step]
    sums = jnp.concatenate(
        [
            jnp.dot(
                total[:, start : start + LANES],
                same,
                precision=lax.Precision.HIGHEST,
                preferred_element_type=jnp.float32,
            )
            for start in range(0, total.shape[1], LANES)
        ],
        axis=1,
    )
    for step, copy in copies:
        copy.wait_send()
    return sums[0:1], sums[1:2]


def folded(values):
    return jnp.sum(values.reshape(-1, 8, values.shape[-1]), axis=0)


def packed_sums(packed, first, second):
    packed[0:1] = jnp.sum(first, axis=0, keepdims=True)
    packed[1:2] = jnp.sum(second, axis=0, keepdims=True)


def norm_kernel(sizes, width, group_size, x_ref, act_ref, stat_ref, packed, slots, sends, recvs):
    barrier, places = greet(*sizes)
    pixels, channels = x_ref.shape
    steps = pixels // CHUNK
    zeros = jnp.zeros((8, channels), jnp.float32)

    def gather(step, carry):
        values = x_ref[pl.ds(step * CHUNK, CHUNK)].astype(jnp.float32)
        return carry[0] + folded(values), carry[1] + folded(values * values)

    packed_sums(packed, *lax.fori_loop(0, steps, gather, (zeros, zeros)))
    total, square_sum = clip_sums(barrier, places, width, packed, slots, sends, recvs)
    average = total / group_size
    inverse_dev = lax.rsqrt(square_sum / group_size - average * average + EPS)
    stat_ref[0:1] = average
    stat_ref[1:2] = inverse_dev

    def apply(step, carry):
        rows = pl.ds(step * CHUNK, CHUNK)
        normed = (x_ref[rows].astype(jnp.float32) - average) * inverse_dev
        act_ref[rows] = (normed * jax.nn.sigmoid(normed)).astype(jnp.bfloat16)
        return carry

    lax.fori_loop(0, steps, apply, 0)


def back_kernel(
    sizes, width, group_size, up_ref, x_ref, stat_ref, out_ref, slope, packed, slots, sends, recvs
):
    barrier, places = greet(*sizes)
    pixels, channels = x_ref.shape
    steps = pixels // CHUNK
    zeros = jnp.zeros((8, channels), jnp.float32)
    average = stat_ref[0:1]
    inverse_dev = stat_ref[1:2]

    def normed_rows(rows):
        return (x_ref[rows].astype(jnp.float32) - average) * inverse_dev

    def gather(step, carry):
        rows = pl.ds(step * CHUNK, CHUNK)
        normed = normed_rows(rows)
        sigmoid_val = jax.nn.sigmoid(normed)
        values = up_ref[rows] * sigmoid_val * (1.0 + normed * (1.0 - sigmoid_val))
        slope[rows] = values
        return carry[0] + folded(values), carry[1] + folded(values * normed)

    packed_sums(packed, *lax.fori_loop(0, steps, gather, (zeros, zeros)))
    sum_grad, sum_cross = clip_sums(barrier, places, width, packed, slots, sends, recvs)
    mean_grad = sum_grad / group_size
    mean_cross = sum_cross / group_size

    def apply(step, carry):
        rows = pl.ds(step * CHUNK, CHUNK)
        centered = slope[rows] - mean_grad - normed_rows(rows) * mean_cross
        out_ref[rows] = (centered * inverse_dev).astype(jnp.bfloat16)
        return carry

    lax.fori_loop(0, steps, apply, 0)


def norm_call(kernel, ident, group_size, operands, out_shape, scratch):
    channels = operands[0].shape[-1]
    sizes = (lax.axis_size("tm"), lax.axis_size("space"))
    peers = sizes[0] * sizes[1]
    return pl.pallas_call(
        functools.partial(kernel, sizes, channels // GROUPS, group_size),
        out_shape=out_shape,
        in_specs=[pl.BlockSpec(memory_space=pltpu.VMEM)] * len(operands),
        out_specs=jax.tree.map(lambda _: pl.BlockSpec(memory_space=pltpu.VMEM), out_shape),
        scratch_shapes=scratch
        + [
            pltpu.VMEM((2, channels), jnp.float32),
            pltpu.VMEM((peers, 2, channels), jnp.float32),
            pltpu.SemaphoreType.DMA((peers,)),
            pltpu.SemaphoreType.DMA((peers,)),
        ],
        compiler_params=pltpu.CompilerParams(collective_id=ident, has_side_effects=True),
    )(*operands)


def norm_forward(field, group_size):
    flat = field.reshape(-1, field.shape[-1])
    out = (
        jax.ShapeDtypeStruct(flat.shape, jnp.bfloat16),
        jax.ShapeDtypeStruct((2, flat.shape[1]), jnp.float32),
    )
    act, stats = norm_call(norm_kernel, 0, group_size, [flat], out, [])
    return act.reshape(field.shape), stats


def norm_backward(upstream, field, stats, group_size):
    flat = field.reshape(-1, field.shape[-1])
    out = jax.ShapeDtypeStruct(flat.shape, jnp.bfloat16)
    scratch = [pltpu.VMEM(flat.shape, jnp.float32)]
    operands = [upstream.reshape(flat.shape), flat, stats]
    grad = norm_call(back_kernel, 1, group_size, operands, out, scratch)
    return grad.reshape(field.shape)


def both_halves(mine):
    if lax.axis_size("dp") != 2:
        return lax.all_gather(mine, "dp", axis=0, tiled=True)
    other = lax.ppermute(mine, "dp", [(0, 1), (1, 0)])
    initial = lax.axis_index("dp") == 0
    return jnp.concatenate(
        [jnp.where(initial, mine, other), jnp.where(initial, other, mine)], axis=0
    )


def axis_bits(axis):
    size = lax.axis_size(axis)
    return [(axis, bit) for bit in reversed(range(size.bit_length() - 1))]


def scattered(terms, order):
    bits = axis_bits("dp") + axis_bits("tm") + axis_bits("space")
    rows, cols = terms.shape
    total = terms.reshape((2,) * len(bits) + (rows >> len(bits), cols))
    left = list(bits)
    for axis, bit in order:
        dim = left.index((axis, bit))
        left.pop(dim)
        mine = (lax.axis_index(axis) >> bit) & 1
        kept = lax.dynamic_index_in_dim(total, mine, dim, keepdims=False)
        sent = lax.dynamic_index_in_dim(total, 1 - mine, dim, keepdims=False)
        pairs = [(i, i ^ (1 << bit)) for i in range(lax.axis_size(axis))]
        got = lax.ppermute(sent.astype(jnp.bfloat16), axis, pairs)
        total = kept + got.astype(jnp.float32)
    return total


def reduce_rows(terms):
    near = list(reversed(axis_bits("space")))
    tm_bits = axis_bits("tm")
    first = axis_bits("dp") + tm_bits + near
    second = axis_bits("dp") + tm_bits[::-1] + near
    return jnp.concatenate([scattered(terms[0], first), scattered(terms[1], second)], axis=1)


def along_time(edge_frames, offset):
    return passed_along(edge_frames, "tm", offset)


def edge_rows_of(field):
    peers = lax.axis_size("space")
    up = [(i, i + 1) for i in range(peers - 1)]
    down = [(j, i) for i, j in up]
    above = lax.ppermute(field[:, -1:], "space", up)
    below = lax.ppermute(field[:, :1], "space", down)
    return above, below


def conv_kernel(back, x_ref, above_ref, below_ref, k_ref, out_ref, shifted, total):
    frames, row_count, cols, channels = x_ref.shape
    column = lax.broadcasted_iota(jnp.int32, (cols, channels), 0)

    def spread(frame, row, values):
        shifted[1, frame, row] = values
        wide = values.astype(jnp.float32)
        left = jnp.where(column == 0, 0.0, pltpu.roll(wide, 1, 0))
        right = jnp.where(column == cols - 1, 0.0, pltpu.roll(wide, cols - 1, 0))
        shifted[0, frame, row] = left.astype(jnp.bfloat16)
        shifted[2, frame, row] = right.astype(jnp.bfloat16)

    for frame in range(frames):
        spread(frame, 0, above_ref[frame, 0])
        spread(frame, row_count + 1, below_ref[frame, 0])

        def one_row(row, carry, frame=frame):
            spread(frame, row + 1, x_ref[frame, row])
            return carry

        lax.fori_loop(0, row_count, one_row, 0)
    contract = (((1,), (1 if back else 0,)), ((), ()))
    flat = row_count * cols
    for frame in range(frames):
        total[...] = jnp.zeros_like(total)

        def one_tap(i, carry, frame=frame):
            terms = total[...]
            for j in range(3):
                window = shifted[j, frame, pl.ds(i, row_count)].reshape(flat, channels)
                tap = 8 - (i * 3 + j) if back else i * 3 + j
                terms = terms + lax.dot_general(
                    window, k_ref[tap], contract, preferred_element_type=jnp.float32
                )
            total[...] = terms
            return carry

        lax.fori_loop(0, 3, one_tap, 0)
        result = total[...].reshape(row_count, cols, channels)
        out_ref[frame] = result.astype(out_ref.dtype)


def conv_frames(field, kernel, back):
    above, below = edge_rows_of(field)
    frames, row_count, cols, channels = field.shape
    shifted_shape = (3, frames, row_count + 2, cols, channels)
    total = pltpu.VMEM((row_count * cols, channels), jnp.float32)
    out = jax.ShapeDtypeStruct(field.shape, jnp.float32 if back else jnp.bfloat16)
    flops = 18 * frames * row_count * cols * channels * channels
    params = dict(
        in_specs=[pl.BlockSpec(memory_space=pltpu.VMEM)] * 4,
        cost_estimate=pl.CostEstimate(flops=flops, bytes_accessed=8 << 20, transcendentals=0),
        compiler_params=pltpu.CompilerParams(vmem_limit_bytes=40 << 20),
    )
    whole = pl.BlockSpec(memory_space=pltpu.VMEM)
    operands = (field, above, below, kernel)
    body = functools.partial(conv_kernel, back)
    if back:
        scratch = [pltpu.VMEM(shifted_shape, jnp.bfloat16), total]
        return pl.pallas_call(
            body, out_shape=out, out_specs=whole, scratch_shapes=scratch, **params
        )(*operands)
    shifted = jax.ShapeDtypeStruct(shifted_shape, jnp.bfloat16)
    return pl.pallas_call(
        body,
        out_shape=(out, shifted),
        out_specs=(whole, whole),
        scratch_shapes=[total],
        **params,
    )(*operands)


def against_rows(left_rows, kernel):
    return lax.dot_general(
        left_rows, kernel, (((1,), (1,)), ((), ())), preferred_element_type=jnp.float32
    )


def over_pixels(left_rows, right_rows):
    return lax.dot_general(
        left_rows, right_rows, (((0,), (0,)), ((), ())), preferred_element_type=jnp.float32
    )


def kernel_grads(windows, flat):
    half = flat.shape[1] // 2
    terms = jnp.concatenate([over_pixels(window, flat) for window in windows], axis=0)
    return reduce_rows((terms[:, :half], terms[:, half:]))


def local(
    features,
    base_spatial,
    delta_spatial,
    keep_spatial,
    base_temporal,
    delta_temporal,
    keep_temporal,
    cotangent,
):
    frames, row_count, col_count, channels = (
        features.shape[1],
        features.shape[2],
        features.shape[3],
        features.shape[4],
    )
    spread_over = lax.axis_size("tm") * lax.axis_size("space")
    group_size = float(frames * row_count * col_count * spread_over * (channels // GROUPS))
    pixels = frames * row_count * col_count
    grad_factor = 1.0 / math.sqrt(pixels * spread_over * lax.axis_size("dp"))
    merged_spatial = (
        base_spatial.astype(jnp.float32)
        + keep_spatial.astype(jnp.float32) * delta_spatial.astype(jnp.float32)
    ).astype(jnp.bfloat16)
    merged_temporal = (
        base_temporal.astype(jnp.float32)
        + keep_temporal.astype(jnp.float32) * delta_temporal.astype(jnp.float32)
    ).astype(jnp.bfloat16)
    full_spatial, full_temporal = both_halves(merged_spatial), both_halves(merged_temporal)
    kernel_space = full_spatial.reshape(9, channels, channels)
    kernel_time = full_temporal.reshape(3, channels, channels)
    inputs = features[0]
    activated, stats_in = norm_forward(inputs, group_size)
    hidden, shifted = conv_frames(activated, kernel_space, False)
    gated_act, stats_mid = norm_forward(hidden, group_size)
    leading = lax.axis_index("tm") == 0
    earlier = along_time(gated_act[frames - 2 :], 1)
    earlier = jnp.where(leading, jnp.broadcast_to(gated_act[0:1], earlier.shape), earlier)
    extended = jnp.concatenate([earlier, gated_act], axis=0).reshape(
        frames + 2, row_count * col_count, channels
    )
    output = jnp.zeros((pixels, channels), jnp.float32)
    for tap_index in range(3):
        output = output + jnp.dot(
            extended[tap_index : tap_index + frames].reshape(pixels, channels),
            kernel_time[tap_index],
            preferred_element_type=jnp.float32,
        )
    decoded = output.reshape(frames, row_count, col_count, channels).astype(jnp.bfloat16)[None]
    upstream = cotangent[0]
    later = along_time(upstream, -1)
    ahead = jnp.concatenate([upstream, later], axis=0).reshape(
        frames + 2, row_count * col_count, channels
    )
    flat_up = upstream.reshape(pixels, channels)
    grad_gated = jnp.zeros((pixels, channels), jnp.float32)
    time_grads = []
    for tap_index in range(3):
        grad_gated = grad_gated + against_rows(
            ahead[2 - tap_index : 2 - tap_index + frames].reshape(pixels, channels),
            kernel_time[tap_index],
        )
        time_grads.append(extended[tap_index : tap_index + frames].reshape(pixels, channels))
    edge_rows = row_count * col_count
    first_up = flat_up[:edge_rows]
    second_up = flat_up[edge_rows : 2 * edge_rows]
    edge_term = (
        against_rows(first_up, kernel_time[0])
        + against_rows(second_up, kernel_time[0])
        + against_rows(first_up, kernel_time[1])
    )
    edge_term = jnp.where(leading, edge_term, 0.0)
    grad_gated = jnp.concatenate(
        [grad_gated[:edge_rows] + edge_term, grad_gated[edge_rows:]], axis=0
    )
    grad_hidden = norm_backward(
        grad_gated.reshape(frames, row_count, col_count, channels), hidden, stats_mid, group_size
    )
    flat_hidden = grad_hidden.reshape(pixels, channels)
    space_grads = []
    for row_shift in range(3):
        for col_shift in range(3):
            window = shifted[col_shift][:, row_shift : row_shift + row_count]
            space_grads.append(window.reshape(pixels, channels))
    grad_act = conv_frames(grad_hidden, kernel_space, True)
    grad_input = norm_backward(grad_act, inputs, stats_in, group_size)[None]
    grad_spatial = kernel_grads(space_grads, flat_hidden) * grad_factor
    grad_temporal = kernel_grads(time_grads, flat_up) * grad_factor
    return (decoded, grad_input, grad_spatial, grad_temporal)


def solution(mesh):
    placed = (
        P("dp", "tm", "space", None, None),
        P("dp", None),
        P("dp", None),
        P("dp", None),
        P("dp", None),
        P("dp", None),
        P("dp", None),
        P("dp", "tm", "space", None, None),
    )
    return jax.shard_map(
        local,
        mesh=mesh,
        in_specs=placed,
        out_specs=(
            P("dp", "tm", "space", None, None),
            P("dp", "tm", "space", None, None),
            P(("dp", "tm", "space"), None),
            P(("dp", "tm", "space"), None),
        ),
        check_vma=False,
    )
```
